128 devices in a mesh: slab: 8 (over z, core), leaf: 16 (over y, x).
Axes of the slice: x: 4, y: 4, z: 4, core: 2. Of those that a mesh axis runs over, the one named last changes fastest.
Arguments:
- sources: float32 [8, 16, 512, 1024], P('slab', 'leaf'), may hold values from -6 to 6
- merge_ops: float32 [4, 8, 16, 512, 1024], P(None, 'slab', 'leaf'), may hold values from -1 to 1
- sweep_ops: float32 [8, 16, 512, 512], P('slab', 'leaf'), may hold values from -1 to 1
Outputs:
- interface: float32 [8, 16, 512, 1024], P('slab', 'leaf')
The draws below stay inside these ranges and needn't reach their ends.
All inputs are finite; a program needn't handle non-finite values.
Results may differ from the reference program's by a relative error of at most 0.00017.
Values sent between devices are 32-bit elements; how exact they have to be, the bound alone decides.
A program may use at most 64 MiB of HBM per device.

```python
import jax
import jax.numpy as jnp
from jax import lax

F = 512
COLS = 1024
LEVELS = 4
SLABS = 8
LEAVES = 16
N_LEAF = 16


def draw_merge_ops(key, part):
    first, second = jax.random.split(jax.random.fold_in(key, 11))
    shape = (LEVELS, SLABS, LEAVES, F, 2 * F)
    noise = jax.random.truncated_normal(second, -4.0, 4.0, shape, jnp.float32) * (0.2 / F ** 0.5)
    coeffs = jax.random.uniform(first, (LEVELS, SLABS, LEAVES, 2, F), jnp.float32, 0.4, 0.8)
    unit = jnp.eye(F, dtype=jnp.float32)
    diagonal = jnp.concatenate([coeffs[:, :, :, 0, :, None] * unit, coeffs[:, :, :, 1, :, None] * unit], axis=-1)
    return noise + diagonal


def draw_sweep_ops(key, part):
    first, second = jax.random.split(jax.random.fold_in(key, 23))
    shape = (SLABS, LEAVES, F, F)
    noise = jax.random.truncated_normal(second, -4.0, 4.0, shape, jnp.float32) * (0.15 / F ** 0.5)
    rates = jnp.exp(jax.random.uniform(first, (SLABS, LEAVES, F), jnp.float32, jnp.log(0.35), jnp.log(0.9)))
    return noise + rates[..., None] * jnp.eye(F, dtype=jnp.float32)


def block_levels(rng, extent, cuts, low, largest):
    level = 1.0
    for position, parts in cuts:
        draws = jax.random.uniform(jax.random.fold_in(jax.random.fold_in(rng, 6), position), (parts,), jnp.float32, low / len(cuts), largest / len(cuts))
        level = level * jnp.repeat(jnp.exp(draws), extent[position] // parts).reshape((-1,) + (1,) * (len(extent) - 1 - position))
    return level


def scatter_about(stream_key, shape, spread, limit, cuts=(), kind=jnp.bfloat16):
    entries = spread * jax.random.normal(stream_key, shape, jnp.float32)
    if cuts:
        entries = entries * block_levels(stream_key, shape, cuts, -0.22, 0.18)
    return jnp.clip(entries, -limit, limit).astype(kind)


def setup_inputs(seed: int = 0) -> dict:
    seeds = jax.random.split(jax.random.key(seed), 4)
    sources = scatter_about(seeds[0], (SLABS, LEAVES, F, COLS), 1.0, 6.0, ((0, 8), (1, 16)), jnp.float32)
    merge_ops = draw_merge_ops(jax.random.fold_in(seeds[3], 71), 0)
    sweep_ops = draw_sweep_ops(jax.random.fold_in(seeds[3], 71), 0)
    return dict(sources=sources, merge_ops=merge_ops, sweep_ops=sweep_ops)


def reference(sources, merge_ops, sweep_ops):
    leaf_bits = N_LEAF.bit_length() - 1
    current = sources
    for level_index in range(LEVELS):
        stride = 2 ** (level_index % leaf_bits)
        partner = current.reshape(SLABS, LEAVES // (2 * stride), 2, stride, F, COLS)[:, :, ::-1].reshape(current.shape)
        stacked = jnp.concatenate([current, partner], axis=2)

        def apply_merge(operands):
            return jnp.einsum("lfg,lgc->lfc", operands[0], operands[1], precision=lax.Precision.HIGHEST)

        current = lax.map(apply_merge, (merge_ops[level_index], stacked))

    def advance(carried, operands):
        updated = jnp.einsum("lfg,lgc->lfc", operands[0], carried + operands[1], precision=lax.Precision.HIGHEST)
        return updated, updated

    start = jnp.zeros((LEAVES, F, COLS), jnp.float32)
    _, interface = lax.scan(advance, start, (sweep_ops, current))
    return interface
```

```python
import functools

import jax
import jax.numpy as jnp
from jax import lax
from jax.experimental import pallas as pl
from jax.experimental.pallas import tpu as pltpu
from jax.sharding import PartitionSpec as P

MESH = pl.DeviceIdType.MESH
F32 = jnp.float32
BF16 = jnp.bfloat16
F = 512
COLS = 1024
LEVELS = 4
CHIPS = 4
BLOCK = 128
C = 64
N = COLS // C
AHEAD = 2


def halves(value):
    high = value.astype(BF16)
    return high, (value - high.astype(F32)).astype(BF16)


def product(left, high, low):
    rows = left.shape[0]
    left_high, left_low = halves(left)
    both = jnp.dot(
        jnp.concatenate([left_high, left_low], axis=0), high, preferred_element_type=F32
    )
    return both[:rows] + both[rows:] + jnp.dot(left_high, low, preferred_element_type=F32)


def kernel(
    src, merge, sweep, out,
    src_stage, merge_stage, sweep_stage, sweep_turned, even_turned,
    state, arrived, from_even, carried, result,
    merge_high, merge_low, sweep_high, sweep_low,
    load_sem, send_sem, recv_sem, even_send, even_recv, op_send, op_recv,
    carry_send, carry_recv,
):
    slab = lax.axis_index("slab")
    leaf = lax.axis_index("leaf")
    z, core = lax.div(slab, 2), lax.rem(slab, 2)
    y, x = lax.div(leaf, 4), lax.rem(leaf, 4)
    partner = (
        (slab, y * 4 + x + 1 - 2 * lax.rem(x, 2)),
        (slab, y * 4 + lax.rem(x + 2, 4)),
        (slab, (y + 1 - 2 * lax.rem(y, 2)) * 4 + x),
        (slab, lax.rem(y + 2, 4) * 4 + x),
    )
    sibling = (slab + 1 - 2 * core, leaf)

    def load_source(block):
        return pltpu.make_async_copy(
            src.at[0, 0, :, pl.ds(pl.multiple_of(block * BLOCK, BLOCK), BLOCK)],
            src_stage.at[block], load_sem.at[block],
        )

    def load_merge(level):
        return pltpu.make_async_copy(
            merge.at[level, 0, 0], merge_stage.at[level], load_sem.at[COLS // BLOCK + level]
        )

    load_sweep = pltpu.make_async_copy(
        sweep.at[0, 0], sweep_stage, load_sem.at[COLS // BLOCK + LEVELS]
    )

    load_source(0).start()
    load_merge(0).start()
    for block in range(1, COLS // BLOCK):
        load_source(block).start()
    for level in range(1, LEVELS):
        load_merge(level).start()
    load_sweep.start()

    barrier = pltpu.get_barrier_semaphore()
    for device in partner + (sibling,):
        pl.semaphore_signal(barrier, inc=1, device_id=device, device_id_type=MESH)

    @pl.when(z > 0)
    def _():
        pl.semaphore_signal(
            barrier, inc=1, device_id=(2 * (z - 1) + 1, leaf), device_id_type=MESH
        )

    below = lax.div(z + 1, CHIPS)
    pl.semaphore_wait(barrier, 5 + 2 * core * (1 - below))

    def rows(chunk):
        return pl.ds(pl.multiple_of(chunk * C, C), C)

    def exchange(level, chunk):
        return pltpu.make_async_remote_copy(
            src_ref=state.at[level, rows(chunk)],
            dst_ref=arrived.at[level, rows(chunk)],
            send_sem=send_sem.at[level, chunk],
            recv_sem=recv_sem.at[level, chunk],
            device_id=partner[level],
            device_id_type=MESH,
        )

    def to_odd(chunk):
        return pltpu.make_async_remote_copy(
            src_ref=state.at[LEVELS, rows(chunk)],
            dst_ref=from_even.at[rows(chunk)],
            send_sem=even_send.at[chunk],
            recv_sem=even_recv.at[chunk],
            device_id=sibling,
            device_id_type=MESH,
        )

    operator_copy = pltpu.make_async_remote_copy(
        src_ref=sweep_turned,
        dst_ref=even_turned,
        send_sem=op_send,
        recv_sem=op_recv,
        device_id=sibling,
        device_id_type=MESH,
    )

    def carry(chunk, target):
        return pltpu.make_async_remote_copy(
            src_ref=result.at[rows(chunk)],
            dst_ref=carried.at[rows(chunk)],
            send_sem=carry_send.at[target, chunk],
            recv_sem=carry_recv.at[chunk],
            device_id=(2 * (z + 1) + target, leaf),
            device_id_type=MESH,
        )

    def turn_source(block):
        load_source(block).wait()
        state[0, pl.ds(pl.multiple_of(block * BLOCK, BLOCK), BLOCK)] = src_stage[block].T

    def prepare_merge(level):
        load_merge(level).wait()

        def turn(step, _):
            at = pl.ds(pl.multiple_of(step * BLOCK, BLOCK), BLOCK)
            high, low = halves(merge_stage[level, :, at].T)
            merge_high[level, at] = high
            merge_low[level, at] = low
            return 0

        lax.fori_loop(0, 2 * F // BLOCK, turn, 0)

    def prepare_sweep():
        load_sweep.wait()

        def turn(step, _):
            at = pl.ds(pl.multiple_of(step * BLOCK, BLOCK), BLOCK)
            turned = sweep_stage[:, at].T
            high, low = halves(turned)
            sweep_turned[at] = turned
            sweep_high[at] = high
            sweep_low[at] = low
            return 0

        lax.fori_loop(0, F // BLOCK, turn, 0)

        @pl.when(core == 0)
        def _():
            operator_copy.start()

    def compose_sweep():
        @pl.when(core == 1)
        def _():
            operator_copy.wait_recv()

            def compose(step, _):
                at = pl.ds(pl.multiple_of(step * BLOCK, BLOCK), BLOCK)
                to = pl.ds(pl.multiple_of(F + step * BLOCK, BLOCK), BLOCK)
                high, low = halves(product(even_turned[at], sweep_high[:F], sweep_low[:F]))
                sweep_high[to] = high
                sweep_low[to] = low
                return 0

            lax.fori_loop(0, F // BLOCK, compose, 0)

    turn_source(0)
    for chunk in range(AHEAD):
        exchange(0, chunk).start()
    prepare_merge(0)
    per_block = BLOCK // C

    def step(k, _):
        for level in range(1, LEVELS):
            pl.when(k == level - 1)(functools.partial(prepare_merge, level))
        pl.when(k == LEVELS - 2)(prepare_sweep)
        pl.when(k == LEVELS - 1)(compose_sweep)

        ahead = k + AHEAD

        @pl.when((ahead < N) & (lax.rem(ahead, per_block) == 0))
        def _():
            turn_source(lax.div(ahead, per_block))

        for level in range(LEVELS):
            chunk = k - level

            @pl.when((chunk >= 0) & (chunk < N))
            def _():
                exchange(level, chunk).wait_recv()
                left = jnp.concatenate(
                    [state[level, rows(chunk)], arrived[level, rows(chunk)]], axis=1
                )
                state[level + 1, rows(chunk)] = product(
                    left, merge_high[level], merge_low[level]
                )
                if level < LEVELS - 1:
                    exchange(level + 1, chunk).start()
                else:
                    @pl.when(core == 0)
                    def _():
                        to_odd(chunk).start()

            if level == 0:
                @pl.when(ahead < N)
                def _():
                    exchange(0, ahead).start()

        chunk = k - LEVELS - z
        inside = (chunk >= 0) & (chunk < N)

        @pl.when(inside & (z > 0))
        def _():
            carry(chunk, 0).wait_recv()

        @pl.when(inside & (z == 0))
        def _():
            carried[rows(chunk)] = jnp.zeros((C, F), F32)

        @pl.when(inside & (core == 0))
        def _():
            left = state[LEVELS, rows(chunk)] + carried[rows(chunk)]
            result[rows(chunk)] = product(left, sweep_high[:F], sweep_low[:F])

        @pl.when(inside & (core == 1))
        def _():
            to_odd(chunk).wait_recv()
            left = jnp.concatenate(
                [state[LEVELS, rows(chunk)], from_even[rows(chunk)] + carried[rows(chunk)]],
                axis=1,
            )
            result[rows(chunk)] = product(left, sweep_high[...], sweep_low[...])

            @pl.when(z < CHIPS - 1)
            def _():
                carry(chunk, 1).start()
                carry(chunk, 0).start()

        @pl.when(inside & (lax.rem(chunk, per_block) == per_block - 1))
        def _():
            block = lax.div(chunk, per_block)
            at = pl.ds(pl.multiple_of(block * BLOCK, BLOCK), BLOCK)
            out[:, at] = result[at].T

        return 0

    lax.fori_loop(0, N + LEVELS + CHIPS - 1, step, 0)

    def finish(chunk, _):
        for level in range(LEVELS):
            exchange(level, chunk).wait_send()

        @pl.when(core == 0)
        def _():
            to_odd(chunk).wait_send()

        @pl.when((core == 1) & (z < CHIPS - 1))
        def _():
            carry(chunk, 0).wait_send()
            carry(chunk, 1).wait_send()

        return 0

    lax.fori_loop(0, N, finish, 0)

    @pl.when(core == 0)
    def _():
        operator_copy.wait_send()


def per_device(sources, merge_ops, sweep_ops):
    anywhere = pl.BlockSpec(memory_space=pl.ANY)
    dma = pltpu.SemaphoreType.DMA
    interface = pl.pallas_call(
        kernel,
        out_shape=jax.ShapeDtypeStruct((F, COLS), F32),
        in_specs=[anywhere] * 3,
        out_specs=pl.BlockSpec(memory_space=pltpu.VMEM),
        scratch_shapes=[
            pltpu.VMEM((COLS // BLOCK, F, BLOCK), F32),
            pltpu.VMEM((LEVELS, F, 2 * F), F32),
            pltpu.VMEM((F, F), F32),
            pltpu.VMEM((F, F), F32),
            pltpu.VMEM((F, F), F32),
            pltpu.VMEM((LEVELS + 1, COLS, F), F32),
            pltpu.VMEM((LEVELS, COLS, F), F32),
            pltpu.VMEM((COLS, F), F32),
            pltpu.VMEM((COLS, F), F32),
            pltpu.VMEM((COLS, F), F32),
            pltpu.VMEM((LEVELS, 2 * F, F), BF16),
            pltpu.VMEM((LEVELS, 2 * F, F), BF16),
            pltpu.VMEM((2 * F, F), BF16),
            pltpu.VMEM((2 * F, F), BF16),
            dma((COLS // BLOCK + LEVELS + 1,)),
            dma((LEVELS, N)),
            dma((LEVELS, N)),
            dma((N,)),
            dma((N,)),
            dma,
            dma,
            dma((2, N)),
            dma((N,)),
        ],
        compiler_params=pltpu.CompilerParams(
            collective_id=0, has_side_effects=True, vmem_limit_bytes=60 << 20
        ),
        cost_estimate=pl.CostEstimate(
            flops=3 * 10 * F * F * COLS, bytes_accessed=15 << 20, transcendentals=0
        ),
        name="solve",
    )(sources, merge_ops, sweep_ops)
    return interface[None, None]


def solution(mesh):
    in_specs = (
        P("slab", "leaf", None, None),
        P(None, "slab", "leaf", None, None),
        P("slab", "leaf", None, None),
    )
    out_specs = P("slab", "leaf", None, None)
    return jax.shard_map(
        per_device, mesh=mesh, in_specs=in_specs, out_specs=out_specs, check_vma=False
    )
```

```python
import functools

import jax
import jax.numpy as jnp
from jax import lax
from jax.experimental import pallas as pl
from jax.experimental.pallas import tpu as pltpu
from jax.sharding import PartitionSpec as P

MESH = pl.DeviceIdType.MESH
F32 = jnp.float32
BF16 = jnp.bfloat16
F = 512
COLS = 1024
LEVELS = 4
CHIPS = 4
BLOCK = 128
C = 64
N = COLS // C
AHEAD = 2
PIECES = 2
PIECE = C // PIECES
PARTS = 4


def halves(value):
    high = value.astype(BF16)
    return high, (value - high.astype(F32)).astype(BF16)


def product(left, high, low):
    rows = left.shape[0]
    left_high, left_low = halves(left)
    both = jnp.dot(
        jnp.concatenate([left_high, left_low], axis=0), high, preferred_element_type=F32
    )
    return both[:rows] + both[rows:] + jnp.dot(left_high, low, preferred_element_type=F32)


def kernel(
    src, merge, sweep, out,
    src_stage, merge_stage, sweep_stage, sweep_turned, even_turned,
    state, arrived, from_even, carried, result, out_stage,
    merge_high, merge_low, sweep_high, sweep_low,
    load_sem, send_sem, recv_sem, even_send, even_recv, op_send, op_recv,
    carry_send, carry_recv, pass_send, pass_recv, store_sem,
):
    slab = lax.axis_index("slab")
    leaf = lax.axis_index("leaf")
    z, core = lax.div(slab, 2), lax.rem(slab, 2)
    y, x = lax.div(leaf, 4), lax.rem(leaf, 4)
    partner = (
        (slab, y * 4 + x + 1 - 2 * lax.rem(x, 2)),
        (slab, y * 4 + lax.rem(x + 2, 4)),
        (slab, (y + 1 - 2 * lax.rem(y, 2)) * 4 + x),
        (slab, lax.rem(y + 2, 4) * 4 + x),
    )
    sibling = (slab + 1 - 2 * core, leaf)
    blocks = COLS // BLOCK
    per_block = BLOCK // C

    def at_block(block):
        return pl.ds(pl.multiple_of(block * BLOCK, BLOCK), BLOCK)

    def load_source(block):
        return pltpu.make_async_copy(
            src.at[0, 0, :, at_block(block)], src_stage.at[block], load_sem.at[block]
        )

    def load_merge(level):
        return pltpu.make_async_copy(
            merge.at[level, 0, 0], merge_stage.at[level], load_sem.at[blocks + level]
        )

    load_sweep = pltpu.make_async_copy(
        sweep.at[0, 0], sweep_stage, load_sem.at[blocks + LEVELS]
    )

    load_source(0).start()
    load_merge(0).start()
    for block in range(1, blocks):
        load_source(block).start()
    for level in range(1, LEVELS):
        load_merge(level).start()
    load_sweep.start()

    barrier = pltpu.get_barrier_semaphore()
    for device in partner + (sibling,):
        pl.semaphore_signal(barrier, inc=1, device_id=device, device_id_type=MESH)

    @pl.when((z > 0) & (core == 1))
    def _():
        pl.semaphore_signal(barrier, inc=1, device_id=(slab - 2, leaf), device_id_type=MESH)

    last = lax.div(z + 1, CHIPS)
    pl.semaphore_wait(barrier, 5 + core * (1 - last))

    def rows(chunk):
        return pl.ds(pl.multiple_of(chunk * C, C), C)

    def piece_rows(chunk, piece):
        return pl.ds(pl.multiple_of(chunk * C + piece * PIECE, PIECE), PIECE)

    def exchange(level, chunk):
        return pltpu.make_async_remote_copy(
            src_ref=state.at[level, rows(chunk)],
            dst_ref=arrived.at[level, rows(chunk)],
            send_sem=send_sem.at[level, chunk],
            recv_sem=recv_sem.at[level, chunk],
            device_id=partner[level],
            device_id_type=MESH,
        )

    def to_odd(chunk):
        return pltpu.make_async_remote_copy(
            src_ref=state.at[LEVELS, rows(chunk)],
            dst_ref=from_even.at[rows(chunk)],
            send_sem=even_send.at[chunk],
            recv_sem=even_recv.at[chunk],
            device_id=sibling,
            device_id_type=MESH,
        )

    operator_copy = pltpu.make_async_remote_copy(
        src_ref=sweep_turned,
        dst_ref=even_turned,
        send_sem=op_send,
        recv_sem=op_recv,
        device_id=sibling,
        device_id_type=MESH,
    )

    def carry(chunk, piece):
        return pltpu.make_async_remote_copy(
            src_ref=result.at[piece_rows(chunk, piece)],
            dst_ref=carried.at[piece_rows(chunk, piece)],
            send_sem=carry_send.at[piece, chunk],
            recv_sem=carry_recv.at[piece, chunk],
            device_id=(slab + 2, leaf),
            device_id_type=MESH,
        )

    def pass_on(chunk, piece):
        return pltpu.make_async_remote_copy(
            src_ref=carried.at[piece_rows(chunk, piece)],
            dst_ref=carried.at[piece_rows(chunk, piece)],
            send_sem=pass_send.at[piece, chunk],
            recv_sem=pass_recv.at[piece, chunk],
            device_id=sibling,
            device_id_type=MESH,
        )

    def store(block):
        return pltpu.make_async_copy(
            out_stage.at[block], out.at[:, at_block(block)], store_sem.at[block]
        )

    def turn_source(block):
        load_source(block).wait()
        state[0, at_block(block)] = src_stage[block].T

    def prepare_merge(level):
        load_merge(level).wait()

        def turn(step, _):
            at = at_block(step)
            high, low = halves(merge_stage[level, :, at].T)
            merge_high[level, at] = high
            merge_low[level, at] = low
            return 0

        lax.fori_loop(0, 2 * F // BLOCK, turn, 0)

    def prepare_sweep():
        load_sweep.wait()

        def turn(step, _):
            at = at_block(step)
            to = at_block(F // BLOCK + step)
            turned = sweep_stage[:, at].T
            high, low = halves(turned)
            sweep_turned[at] = turned
            sweep_high[at] = high
            sweep_low[at] = low
            sweep_high[to] = high
            sweep_low[to] = low
            return 0

        lax.fori_loop(0, F // BLOCK, turn, 0)

        @pl.when(core == 0)
        def _():
            operator_copy.start()

    def compose_sweep():
        @pl.when(core == 1)
        def _():
            operator_copy.wait_recv()

            def compose(step, _):
                at = at_block(step)
                to = at_block(F // BLOCK + step)
                high, low = halves(product(even_turned[at], sweep_high[:F], sweep_low[:F]))
                sweep_high[to] = high
                sweep_low[to] = low
                return 0

            lax.fori_loop(0, F // BLOCK, compose, 0)

    for block in range(-(-AHEAD * C // BLOCK)):
        turn_source(block)
    for chunk in range(AHEAD):
        exchange(0, chunk).start()
    prepare_merge(0)

    def step(k, _):
        for level in range(1, LEVELS):
            pl.when(k == level - 1)(functools.partial(prepare_merge, level))
        pl.when(k == LEVELS - 2)(prepare_sweep)
        pl.when(k == LEVELS - 1)(compose_sweep)

        ahead = k + AHEAD

        @pl.when((ahead < N) & (lax.rem(ahead, per_block) == 0))
        def _():
            turn_source(lax.div(ahead, per_block))

        for level in range(LEVELS):
            chunk = k - level

            @pl.when((chunk >= 0) & (chunk < N))
            def _():
                own = product(
                    state[level, rows(chunk)], merge_high[level, :F], merge_low[level, :F]
                )
                exchange(level, chunk).wait_recv()
                state[level + 1, rows(chunk)] = own + product(
                    arrived[level, rows(chunk)], merge_high[level, F:], merge_low[level, F:]
                )
                if level < LEVELS - 1:
                    exchange(level + 1, chunk).start()
                else:
                    @pl.when(core == 0)
                    def _():
                        to_odd(chunk).start()

                if level > 0:
                    exchange(level - 1, chunk).wait_send()

            if level == 0:
                @pl.when(ahead < N)
                def _():
                    exchange(0, ahead).start()

        chunk = k - LEVELS

        @pl.when((chunk >= 0) & (chunk < N))
        def _():
            result[rows(chunk)] = product(
                state[LEVELS, rows(chunk)], sweep_high[:F], sweep_low[:F]
            )

            @pl.when(core == 1)
            def _():
                to_odd(chunk).wait_recv()
                result[rows(chunk)] += product(
                    from_even[rows(chunk)], sweep_high[F:], sweep_low[F:]
                )

                @pl.when(z == 0)
                def _():
                    for piece in range(PIECES):
                        carry(chunk, piece).start()

            exchange(LEVELS - 1, chunk).wait_send()

            @pl.when(core == 0)
            def _():
                to_odd(chunk).wait_send()

        chunk = k - LEVELS - z
        inside = (chunk >= 0) & (chunk < N)

        @pl.when(inside & (z > 0))
        def _():
            for piece in range(PIECES):
                @pl.when(core == 1)
                def _():
                    carry(chunk, piece).wait_recv()
                    pass_on(chunk, piece).start()

                @pl.when(core == 0)
                def _():
                    pass_on(chunk, piece).wait_recv()

                at = piece_rows(chunk, piece)
                result[at] += product(carried[at], sweep_high[F:], sweep_low[F:])

                @pl.when((core == 1) & (z < CHIPS - 1))
                def _():
                    carry(chunk, piece).start()

        @pl.when(inside & (lax.rem(chunk, per_block) == per_block - 1))
        def _():
            block = lax.div(chunk, per_block)
            out_stage[block] = result[at_block(block)].T
            store(block).start()

        def settle(chunk):
            for piece in range(PIECES):
                @pl.when((core == 1) & (z < CHIPS - 1))
                def _():
                    carry(chunk, piece).wait_send()

                @pl.when((core == 1) & (z > 0))
                def _():
                    pass_on(chunk, piece).wait_send()

        @pl.when((chunk >= 1) & (chunk < N))
        def _():
            settle(chunk - 1)

        @pl.when(chunk == N - 1)
        def _():
            settle(chunk)

        return 0

    lax.fori_loop(0, N + LEVELS + z, step, 0)

    @pl.when(core == 0)
    def _():
        operator_copy.wait_send()

    for block in range(blocks):
        store(block).wait()


def hand_over(given, out, stage, in_sem, out_sem):
    parts = stage.shape[0]

    def move_in(part):
        return pltpu.make_async_copy(
            given.at[pl.ds(part * (F // parts), F // parts)], stage.at[part], in_sem.at[part]
        )

    def move_out(part):
        return pltpu.make_async_copy(
            stage.at[part], out.at[pl.ds(part * (F // parts), F // parts)], out_sem.at[part]
        )

    for part in range(parts):
        move_in(part).start()
    for part in range(parts):
        move_in(part).wait()
        move_out(part).start()
    for part in range(parts):
        move_out(part).wait()


def per_device(sources, merge_ops, sweep_ops):
    anywhere = pl.BlockSpec(memory_space=pl.ANY)
    dma = pltpu.SemaphoreType.DMA
    whole = pltpu.VMEM((COLS, F), F32)
    square = pltpu.VMEM((F, F), F32)
    blocks = COLS // BLOCK
    interface = pl.pallas_call(
        kernel,
        out_shape=jax.ShapeDtypeStruct((F, COLS), F32),
        in_specs=[anywhere] * 3,
        out_specs=anywhere,
        scratch_shapes=[
            pltpu.VMEM((blocks, F, BLOCK), F32),
            pltpu.VMEM((LEVELS, F, 2 * F), F32),
            square,
            square,
            square,
            pltpu.VMEM((LEVELS + 1, COLS, F), F32),
            pltpu.VMEM((LEVELS, COLS, F), F32),
            whole,
            whole,
            whole,
            pltpu.VMEM((blocks, F, BLOCK), F32),
            pltpu.VMEM((LEVELS, 2 * F, F), BF16),
            pltpu.VMEM((LEVELS, 2 * F, F), BF16),
            pltpu.VMEM((2 * F, F), BF16),
            pltpu.VMEM((2 * F, F), BF16),
            dma((blocks + LEVELS + 1,)),
            dma((LEVELS, N)),
            dma((LEVELS, N)),
            dma((N,)),
            dma((N,)),
            dma,
            dma,
            dma((PIECES, N)),
            dma((PIECES, N)),
            dma((PIECES, N)),
            dma((PIECES, N)),
            dma((blocks,)),
        ],
        compiler_params=pltpu.CompilerParams(
            collective_id=0, has_side_effects=True, vmem_limit_bytes=60 << 20
        ),
        cost_estimate=pl.CostEstimate(
            flops=3 * 10 * F * F * COLS, bytes_accessed=15 << 20, transcendentals=0
        ),
        name="solve",
    )(sources, merge_ops, sweep_ops)
    interface = pl.pallas_call(
        hand_over,
        out_shape=jax.ShapeDtypeStruct((F, COLS), F32),
        in_specs=[anywhere],
        out_specs=anywhere,
        scratch_shapes=[pltpu.VMEM((PARTS, F // PARTS, COLS), F32), dma((PARTS,)), dma((PARTS,))],
        name="hand_over",
    )(interface)
    return interface[None, None]


def solution(mesh):
    in_specs = (
        P("slab", "leaf", None, None),
        P(None, "slab", "leaf", None, None),
        P("slab", "leaf", None, None),
    )
    out_specs = P("slab", "leaf", None, None)
    return jax.shard_map(
        per_device, mesh=mesh, in_specs=in_specs, out_specs=out_specs, check_vma=False
    )
```

```python
import functools

import jax
import jax.numpy as jnp
from jax import lax
from jax.experimental import pallas as pl
from jax.experimental.pallas import tpu as pltpu
from jax.sharding import PartitionSpec as P

MESH = pl.DeviceIdType.MESH
F32 = jnp.float32
BF16 = jnp.bfloat16
F = 512
COLS = 1024
LEVELS = 4
CHIPS = 4
BLOCK = 128
C = 64
N = COLS // C
AHEAD = 2
PIECES = 2
PIECE = C // PIECES


def halves(value):
    high = value.astype(BF16)
    return high, (value - high.astype(F32)).astype(BF16)


def product(left, high, low):
    rows = left.shape[0]
    left_high, left_low = halves(left)
    both = jnp.dot(
        jnp.concatenate([left_high, left_low], axis=0), high, preferred_element_type=F32
    )
    return both[:rows] + both[rows:] + jnp.dot(left_high, low, preferred_element_type=F32)


def kernel(
    src, merge, sweep, out,
    src_stage, merge_stage, sweep_stage, sweep_turned, even_turned,
    state, arrived, from_even, carried, result, out_stage,
    merge_high, merge_low, sweep_high, sweep_low,
    load_sem, send_sem, recv_sem, even_send, even_recv, op_send, op_recv,
    carry_send, carry_recv, pass_send, pass_recv, store_sem,
):
    slab = lax.axis_index("slab")
    leaf = lax.axis_index("leaf")
    z, core = lax.div(slab, 2), lax.rem(slab, 2)
    y, x = lax.div(leaf, 4), lax.rem(leaf, 4)
    partner = (
        (slab, y * 4 + x + 1 - 2 * lax.rem(x, 2)),
        (slab, y * 4 + lax.rem(x + 2, 4)),
        (slab, (y + 1 - 2 * lax.rem(y, 2)) * 4 + x),
        (slab, lax.rem(y + 2, 4) * 4 + x),
    )
    sibling = (slab + 1 - 2 * core, leaf)
    blocks = COLS // BLOCK
    per_block = BLOCK // C

    def at_block(block):
        return pl.ds(pl.multiple_of(block * BLOCK, BLOCK), BLOCK)

    def load_source(block):
        return pltpu.make_async_copy(
            src.at[0, 0, :, at_block(block)], src_stage.at[block], load_sem.at[block]
        )

    def load_merge(level):
        return pltpu.make_async_copy(
            merge.at[level, 0, 0], merge_stage.at[level], load_sem.at[blocks + level]
        )

    load_sweep = pltpu.make_async_copy(
        sweep.at[0, 0], sweep_stage, load_sem.at[blocks + LEVELS]
    )

    load_source(0).start()
    load_merge(0).start()
    for block in range(1, blocks):
        load_source(block).start()
    for level in range(1, LEVELS):
        load_merge(level).start()
    load_sweep.start()

    barrier = pltpu.get_barrier_semaphore()
    for device in partner + (sibling,):
        pl.semaphore_signal(barrier, inc=1, device_id=device, device_id_type=MESH)

    @pl.when((z > 0) & (core == 1))
    def _():
        pl.semaphore_signal(barrier, inc=1, device_id=(slab - 2, leaf), device_id_type=MESH)

    last = lax.div(z + 1, CHIPS)
    pl.semaphore_wait(barrier, 5 + core * (1 - last))

    def rows(chunk):
        return pl.ds(pl.multiple_of(chunk * C, C), C)

    def piece_rows(chunk, piece):
        return pl.ds(pl.multiple_of(chunk * C + piece * PIECE, PIECE), PIECE)

    def exchange(level, chunk):
        return pltpu.make_async_remote_copy(
            src_ref=state.at[level, rows(chunk)],
            dst_ref=arrived.at[level, rows(chunk)],
            send_sem=send_sem.at[level, chunk],
            recv_sem=recv_sem.at[level, chunk],
            device_id=partner[level],
            device_id_type=MESH,
        )

    def to_odd(chunk):
        return pltpu.make_async_remote_copy(
            src_ref=state.at[LEVELS, rows(chunk)],
            dst_ref=from_even.at[rows(chunk)],
            send_sem=even_send.at[chunk],
            recv_sem=even_recv.at[chunk],
            device_id=sibling,
            device_id_type=MESH,
        )

    operator_copy = pltpu.make_async_remote_copy(
        src_ref=sweep_turned,
        dst_ref=even_turned,
        send_sem=op_send,
        recv_sem=op_recv,
        device_id=sibling,
        device_id_type=MESH,
    )

    def carry(chunk, piece):
        return pltpu.make_async_remote_copy(
            src_ref=result.at[piece_rows(chunk, piece)],
            dst_ref=carried.at[piece_rows(chunk, piece)],
            send_sem=carry_send.at[piece, chunk],
            recv_sem=carry_recv.at[piece, chunk],
            device_id=(slab + 2, leaf),
            device_id_type=MESH,
        )

    def pass_on(chunk, piece):
        return pltpu.make_async_remote_copy(
            src_ref=carried.at[piece_rows(chunk, piece)],
            dst_ref=carried.at[piece_rows(chunk, piece)],
            send_sem=pass_send.at[piece, chunk],
            recv_sem=pass_recv.at[piece, chunk],
            device_id=sibling,
            device_id_type=MESH,
        )

    def store(block):
        return pltpu.make_async_copy(
            out_stage.at[block], out.at[:, at_block(block)], store_sem.at[block]
        )

    def turn_source(block):
        load_source(block).wait()
        state[0, at_block(block)] = src_stage[block].T

    def prepare_merge(level):
        load_merge(level).wait()

        def turn(step, _):
            at = at_block(step)
            high, low = halves(merge_stage[level, :, at].T)
            merge_high[level, at] = high
            merge_low[level, at] = low
            return 0

        lax.fori_loop(0, 2 * F // BLOCK, turn, 0)

    def prepare_sweep():
        load_sweep.wait()

        def turn(step, _):
            at = at_block(step)
            to = at_block(F // BLOCK + step)
            turned = sweep_stage[:, at].T
            high, low = halves(turned)
            sweep_turned[at] = turned
            sweep_high[at] = high
            sweep_low[at] = low
            sweep_high[to] = high
            sweep_low[to] = low
            return 0

        lax.fori_loop(0, F // BLOCK, turn, 0)

        @pl.when(core == 0)
        def _():
            operator_copy.start()

    def compose_sweep():
        @pl.when(core == 1)
        def _():
            operator_copy.wait_recv()

            def compose(step, _):
                at = at_block(step)
                to = at_block(F // BLOCK + step)
                high, low = halves(product(even_turned[at], sweep_high[:F], sweep_low[:F]))
                sweep_high[to] = high
                sweep_low[to] = low
                return 0

            lax.fori_loop(0, F // BLOCK, compose, 0)

    for block in range(-(-AHEAD * C // BLOCK)):
        turn_source(block)
    for chunk in range(AHEAD):
        exchange(0, chunk).start()
    prepare_merge(0)

    def step(k, _):
        for level in range(1, LEVELS):
            pl.when(k == level - 1)(functools.partial(prepare_merge, level))
        pl.when(k == LEVELS - 2)(prepare_sweep)
        pl.when(k == LEVELS - 1)(compose_sweep)

        ahead = k + AHEAD

        @pl.when((ahead < N) & (lax.rem(ahead, per_block) == 0))
        def _():
            turn_source(lax.div(ahead, per_block))

        for level in range(LEVELS):
            chunk = k - level

            @pl.when((chunk >= 0) & (chunk < N))
            def _():
                own = product(
                    state[level, rows(chunk)], merge_high[level, :F], merge_low[level, :F]
                )
                exchange(level, chunk).wait_recv()
                state[level + 1, rows(chunk)] = own + product(
                    arrived[level, rows(chunk)], merge_high[level, F:], merge_low[level, F:]
                )
                if level < LEVELS - 1:
                    exchange(level + 1, chunk).start()
                else:
                    @pl.when(core == 0)
                    def _():
                        to_odd(chunk).start()

                if level > 0:
                    exchange(level - 1, chunk).wait_send()

            if level == 0:
                @pl.when(ahead < N)
                def _():
                    exchange(0, ahead).start()

        chunk = k - LEVELS

        @pl.when((chunk >= 0) & (chunk < N))
        def _():
            result[rows(chunk)] = product(
                state[LEVELS, rows(chunk)], sweep_high[:F], sweep_low[:F]
            )

            @pl.when(core == 1)
            def _():
                to_odd(chunk).wait_recv()
                result[rows(chunk)] += product(
                    from_even[rows(chunk)], sweep_high[F:], sweep_low[F:]
                )

                @pl.when(z == 0)
                def _():
                    for piece in range(PIECES):
                        carry(chunk, piece).start()

            exchange(LEVELS - 1, chunk).wait_send()

            @pl.when(core == 0)
            def _():
                to_odd(chunk).wait_send()

        chunk = k - LEVELS - z
        inside = (chunk >= 0) & (chunk < N)

        @pl.when(inside & (z > 0))
        def _():
            for piece in range(PIECES):
                @pl.when(core == 1)
                def _():
                    carry(chunk, piece).wait_recv()
                    pass_on(chunk, piece).start()

                @pl.when(core == 0)
                def _():
                    pass_on(chunk, piece).wait_recv()

                at = piece_rows(chunk, piece)
                result[at] += product(carried[at], sweep_high[F:], sweep_low[F:])

                @pl.when((core == 1) & (z < CHIPS - 1))
                def _():
                    carry(chunk, piece).start()

        @pl.when(inside & (lax.rem(chunk, per_block) == per_block - 1))
        def _():
            block = lax.div(chunk, per_block)
            out_stage[block] = result[at_block(block)].T
            store(block).start()

        def settle(chunk):
            for piece in range(PIECES):
                @pl.when((core == 1) & (z < CHIPS - 1))
                def _():
                    carry(chunk, piece).wait_send()

                @pl.when((core == 1) & (z > 0))
                def _():
                    pass_on(chunk, piece).wait_send()

        @pl.when((chunk >= 1) & (chunk < N))
        def _():
            settle(chunk - 1)

        @pl.when(chunk == N - 1)
        def _():
            settle(chunk)

        return 0

    lax.fori_loop(0, N + LEVELS + z, step, 0)

    @pl.when(core == 0)
    def _():
        operator_copy.wait_send()

    for block in range(blocks):
        store(block).wait()


def per_device(sources, merge_ops, sweep_ops):
    anywhere = pl.BlockSpec(memory_space=pl.ANY)
    dma = pltpu.SemaphoreType.DMA
    whole = pltpu.VMEM((COLS, F), F32)
    square = pltpu.VMEM((F, F), F32)
    blocks = COLS // BLOCK
    interface = pl.pallas_call(
        kernel,
        out_shape=jax.ShapeDtypeStruct((F, COLS), F32),
        in_specs=[pl.BlockSpec(memory_space=pltpu.HBM)] * 3,
        out_specs=anywhere,
        scratch_shapes=[
            pltpu.VMEM((blocks, F, BLOCK), F32),
            pltpu.VMEM((LEVELS, F, 2 * F), F32),
            square,
            square,
            square,
            pltpu.VMEM((LEVELS + 1, COLS, F), F32),
            pltpu.VMEM((LEVELS, COLS, F), F32),
            whole,
            whole,
            whole,
            pltpu.VMEM((blocks, F, BLOCK), F32),
            pltpu.VMEM((LEVELS, 2 * F, F), BF16),
            pltpu.VMEM((LEVELS, 2 * F, F), BF16),
            pltpu.VMEM((2 * F, F), BF16),
            pltpu.VMEM((2 * F, F), BF16),
            dma((blocks + LEVELS + 1,)),
            dma((LEVELS, N)),
            dma((LEVELS, N)),
            dma((N,)),
            dma((N,)),
            dma,
            dma,
            dma((PIECES, N)),
            dma((PIECES, N)),
            dma((PIECES, N)),
            dma((PIECES, N)),
            dma((blocks,)),
        ],
        compiler_params=pltpu.CompilerParams(
            collective_id=0, has_side_effects=True, vmem_limit_bytes=50 << 20
        ),
        cost_estimate=pl.CostEstimate(
            flops=3 * 10 * F * F * COLS, bytes_accessed=15 << 20, transcendentals=0
        ),
        name="solve",
    )(*(pltpu.with_memory_space_constraint(each, pltpu.HBM) for each in (sources, merge_ops, sweep_ops)))
    return interface[None, None]


def solution(mesh):
    in_specs = (
        P("slab", "leaf", None, None),
        P(None, "slab", "leaf", None, None),
        P("slab", "leaf", None, None),
    )
    out_specs = P("slab", "leaf", None, None)
    return jax.shard_map(
        per_device, mesh=mesh, in_specs=in_specs, out_specs=out_specs, check_vma=False
    )
```

```python
import functools

import jax
import jax.numpy as jnp
from jax import lax
from jax.experimental import pallas as pl
from jax.experimental.pallas import tpu as pltpu
from jax.sharding import PartitionSpec as P

MESH = pl.DeviceIdType.MESH
F32 = jnp.float32
BF16 = jnp.bfloat16
F = 512
COLS = 1024
LEVELS = 4
CHIPS = 4
BLOCK = 128
C = 64
N = COLS // C
AHEAD = 2
PIECES = 2
PIECE = C // PIECES


def halves(value):
    high = value.astype(BF16)
    return high, (value - high.astype(F32)).astype(BF16)


def product(left, high, low):
    rows = left.shape[0]
    left_high, left_low = halves(left)
    both = jnp.dot(
        jnp.concatenate([left_high, left_low], axis=0), high, preferred_element_type=F32
    )
    return both[:rows] + both[rows:] + jnp.dot(left_high, low, preferred_element_type=F32)


def kernel(
    src, merge, sweep, out,
    src_stage, merge_stage, sweep_stage, sweep_turned, even_turned,
    state, arrived, from_even, carried, result, out_stage,
    merge_high, merge_low, sweep_high, sweep_low,
    load_sem, send_sem, recv_sem, even_send, even_recv, op_send, op_recv,
    carry_send, carry_recv, pass_send, pass_recv, store_sem,
):
    slab = lax.axis_index("slab")
    leaf = lax.axis_index("leaf")
    z, core = lax.div(slab, 2), lax.rem(slab, 2)
    y, x = lax.div(leaf, 4), lax.rem(leaf, 4)
    partner = (
        (slab, y * 4 + x + 1 - 2 * lax.rem(x, 2)),
        (slab, y * 4 + lax.rem(x + 2, 4)),
        (slab, (y + 1 - 2 * lax.rem(y, 2)) * 4 + x),
        (slab, lax.rem(y + 2, 4) * 4 + x),
    )
    sibling = (slab + 1 - 2 * core, leaf)
    late = 1 - core
    blocks = COLS // BLOCK
    per_block = BLOCK // C

    def at_block(block):
        return pl.ds(pl.multiple_of(block * BLOCK, BLOCK), BLOCK)

    def load_source(block):
        return pltpu.make_async_copy(
            src.at[0, 0, :, at_block(block)], src_stage.at[block], load_sem.at[block]
        )

    def load_merge(level):
        return pltpu.make_async_copy(
            merge.at[level, 0, 0], merge_stage.at[level], load_sem.at[blocks + level]
        )

    load_sweep = pltpu.make_async_copy(
        sweep.at[0, 0], sweep_stage, load_sem.at[blocks + LEVELS]
    )

    load_source(0).start()
    load_merge(0).start()
    for block in range(1, blocks):
        load_source(block).start()
    for level in range(1, LEVELS):
        load_merge(level).start()
    load_sweep.start()

    barrier = pltpu.get_barrier_semaphore()
    for device in partner + (sibling,):
        pl.semaphore_signal(barrier, inc=1, device_id=device, device_id_type=MESH)

    @pl.when((z > 0) & (core == 1))
    def _():
        pl.semaphore_signal(barrier, inc=1, device_id=(slab - 2, leaf), device_id_type=MESH)

    last = lax.div(z + 1, CHIPS)
    pl.semaphore_wait(barrier, 5 + core * (1 - last))

    def rows(chunk):
        return pl.ds(pl.multiple_of(chunk * C, C), C)

    def piece_rows(chunk, piece):
        return pl.ds(pl.multiple_of(chunk * C + piece * PIECE, PIECE), PIECE)

    def exchange(level, chunk):
        return pltpu.make_async_remote_copy(
            src_ref=state.at[level, rows(chunk)],
            dst_ref=arrived.at[level, rows(chunk)],
            send_sem=send_sem.at[level, chunk],
            recv_sem=recv_sem.at[level, chunk],
            device_id=partner[level],
            device_id_type=MESH,
        )

    def to_odd(chunk):
        return pltpu.make_async_remote_copy(
            src_ref=state.at[LEVELS, rows(chunk)],
            dst_ref=from_even.at[rows(chunk)],
            send_sem=even_send.at[chunk],
            recv_sem=even_recv.at[chunk],
            device_id=sibling,
            device_id_type=MESH,
        )

    operator_copy = pltpu.make_async_remote_copy(
        src_ref=sweep_turned,
        dst_ref=even_turned,
        send_sem=op_send,
        recv_sem=op_recv,
        device_id=sibling,
        device_id_type=MESH,
    )

    def carry(chunk, piece):
        return pltpu.make_async_remote_copy(
            src_ref=result.at[piece_rows(chunk, piece)],
            dst_ref=carried.at[piece_rows(chunk, piece)],
            send_sem=carry_send.at[piece, chunk],
            recv_sem=carry_recv.at[piece, chunk],
            device_id=(slab + 2, leaf),
            device_id_type=MESH,
        )

    def pass_on(chunk, piece):
        return pltpu.make_async_remote_copy(
            src_ref=carried.at[piece_rows(chunk, piece)],
            dst_ref=carried.at[piece_rows(chunk, piece)],
            send_sem=pass_send.at[piece, chunk],
            recv_sem=pass_recv.at[piece, chunk],
            device_id=sibling,
            device_id_type=MESH,
        )

    def store(block):
        return pltpu.make_async_copy(
            out_stage.at[block], out.at[:, at_block(block)], store_sem.at[block]
        )

    def turn_source(block):
        load_source(block).wait()
        state[0, at_block(block)] = src_stage[block].T

    def prepare_merge(level):
        load_merge(level).wait()

        def turn(step, _):
            at = at_block(step)
            high, low = halves(merge_stage[level, :, at].T)
            merge_high[level, at] = high
            merge_low[level, at] = low
            return 0

        lax.fori_loop(0, 2 * F // BLOCK, turn, 0)

    def prepare_sweep():
        load_sweep.wait()

        def turn(step, _):
            at = at_block(step)
            to = at_block(F // BLOCK + step)
            turned = sweep_stage[:, at].T
            high, low = halves(turned)
            sweep_turned[at] = turned
            sweep_high[at] = high
            sweep_low[at] = low
            sweep_high[to] = high
            sweep_low[to] = low
            return 0

        lax.fori_loop(0, F // BLOCK, turn, 0)

        @pl.when(core == 0)
        def _():
            operator_copy.start()

    def compose_sweep():
        @pl.when(core == 1)
        def _():
            operator_copy.wait_recv()

            def compose(step, _):
                at = at_block(step)
                to = at_block(F // BLOCK + step)
                high, low = halves(product(even_turned[at], sweep_high[:F], sweep_low[:F]))
                sweep_high[to] = high
                sweep_low[to] = low
                return 0

            lax.fori_loop(0, F // BLOCK, compose, 0)

    for block in range(-(-AHEAD * C // BLOCK)):
        turn_source(block)
    for chunk in range(AHEAD):
        exchange(0, chunk).start()
    prepare_merge(0)

    def step(k, _):
        for level in range(1, LEVELS):
            pl.when(k == level - 1)(functools.partial(prepare_merge, level))
        pl.when(k == LEVELS - 2)(prepare_sweep)
        pl.when(k == LEVELS - 1)(compose_sweep)

        ahead = k + AHEAD

        @pl.when((ahead < N) & (lax.rem(ahead, per_block) == 0))
        def _():
            turn_source(lax.div(ahead, per_block))

        for level in range(LEVELS):
            chunk = k - level - late * (level // (LEVELS - 1))

            @pl.when((chunk >= 0) & (chunk < N))
            def _():
                own = product(
                    state[level, rows(chunk)], merge_high[level, :F], merge_low[level, :F]
                )
                exchange(level, chunk).wait_recv()
                state[level + 1, rows(chunk)] = own + product(
                    arrived[level, rows(chunk)], merge_high[level, F:], merge_low[level, F:]
                )
                if level < LEVELS - 1:
                    exchange(level + 1, chunk).start()
                else:
                    @pl.when(core == 0)
                    def _():
                        to_odd(chunk).start()

                if level > 0:
                    exchange(level - 1, chunk).wait_send()

            if level == 0:
                @pl.when(ahead < N)
                def _():
                    exchange(0, ahead).start()

        chunk = k - LEVELS - late

        @pl.when((chunk >= 0) & (chunk < N))
        def _():
            result[rows(chunk)] = product(
                state[LEVELS, rows(chunk)], sweep_high[:F], sweep_low[:F]
            )

            @pl.when(core == 1)
            def _():
                to_odd(chunk).wait_recv()
                result[rows(chunk)] += product(
                    from_even[rows(chunk)], sweep_high[F:], sweep_low[F:]
                )

                @pl.when(z == 0)
                def _():
                    for piece in range(PIECES):
                        carry(chunk, piece).start()

            exchange(LEVELS - 1, chunk).wait_send()

            @pl.when(core == 0)
            def _():
                to_odd(chunk).wait_send()

        chunk = k - LEVELS - late - z
        inside = (chunk >= 0) & (chunk < N)

        @pl.when(inside & (z > 0))
        def _():
            for piece in range(PIECES):
                @pl.when(core == 1)
                def _():
                    carry(chunk, piece).wait_recv()
                    pass_on(chunk, piece).start()

                @pl.when(core == 0)
                def _():
                    pass_on(chunk, piece).wait_recv()

                at = piece_rows(chunk, piece)
                result[at] += product(carried[at], sweep_high[F:], sweep_low[F:])

                @pl.when((core == 1) & (z < CHIPS - 1))
                def _():
                    carry(chunk, piece).start()

        @pl.when(inside & (lax.rem(chunk, per_block) == per_block - 1))
        def _():
            block = lax.div(chunk, per_block)
            out_stage[block] = result[at_block(block)].T
            store(block).start()

        def settle(chunk):
            for piece in range(PIECES):
                @pl.when((core == 1) & (z < CHIPS - 1))
                def _():
                    carry(chunk, piece).wait_send()

                @pl.when((core == 1) & (z > 0))
                def _():
                    pass_on(chunk, piece).wait_send()

        @pl.when((chunk >= 1) & (chunk < N))
        def _():
            settle(chunk - 1)

        @pl.when(chunk == N - 1)
        def _():
            settle(chunk)

        return 0

    lax.fori_loop(0, N + LEVELS + late + z, step, 0)

    @pl.when(core == 0)
    def _():
        operator_copy.wait_send()

    for block in range(blocks):
        store(block).wait()


def per_device(sources, merge_ops, sweep_ops):
    anywhere = pl.BlockSpec(memory_space=pl.ANY)
    dma = pltpu.SemaphoreType.DMA
    whole = pltpu.VMEM((COLS, F), F32)
    square = pltpu.VMEM((F, F), F32)
    blocks = COLS // BLOCK
    interface = pl.pallas_call(
        kernel,
        out_shape=jax.ShapeDtypeStruct((F, COLS), F32),
        in_specs=[pl.BlockSpec(memory_space=pltpu.HBM)] * 3,
        out_specs=anywhere,
        scratch_shapes=[
            pltpu.VMEM((blocks, F, BLOCK), F32),
            pltpu.VMEM((LEVELS, F, 2 * F), F32),
            square,
            square,
            square,
            pltpu.VMEM((LEVELS + 1, COLS, F), F32),
            pltpu.VMEM((LEVELS, COLS, F), F32),
            whole,
            whole,
            whole,
            pltpu.VMEM((blocks, F, BLOCK), F32),
            pltpu.VMEM((LEVELS, 2 * F, F), BF16),
            pltpu.VMEM((LEVELS, 2 * F, F), BF16),
            pltpu.VMEM((2 * F, F), BF16),
            pltpu.VMEM((2 * F, F), BF16),
            dma((blocks + LEVELS + 1,)),
            dma((LEVELS, N)),
            dma((LEVELS, N)),
            dma((N,)),
            dma((N,)),
            dma,
            dma,
            dma((PIECES, N)),
            dma((PIECES, N)),
            dma((PIECES, N)),
            dma((PIECES, N)),
            dma((blocks,)),
        ],
        compiler_params=pltpu.CompilerParams(
            collective_id=0, has_side_effects=True, vmem_limit_bytes=50 << 20
        ),
        cost_estimate=pl.CostEstimate(
            flops=3 * 10 * F * F * COLS, bytes_accessed=15 << 20, transcendentals=0
        ),
        name="solve",
    )(*(pltpu.with_memory_space_constraint(each, pltpu.HBM) for each in (sources, merge_ops, sweep_ops)))
    return interface[None, None]


def solution(mesh):
    in_specs = (
        P("slab", "leaf", None, None),
        P(None, "slab", "leaf", None, None),
        P("slab", "leaf", None, None),
    )
    out_specs = P("slab", "leaf", None, None)
    return jax.shard_map(
        per_device, mesh=mesh, in_specs=in_specs, out_specs=out_specs, check_vma=False
    )
```

```python
import functools

import jax
import jax.numpy as jnp
from jax import lax
from jax.experimental import pallas as pl
from jax.experimental.pallas import tpu as pltpu
from jax.sharding import PartitionSpec as P

MESH = pl.DeviceIdType.MESH
F32 = jnp.float32
BF16 = jnp.bfloat16
F = 512
COLS = 1024
LEVELS = 4
CHIPS = 4
BLOCK = 128
C = 64
N = COLS // C
AHEAD = 2
PIECES = 2
PIECE = C // PIECES


def halves(value):
    high = value.astype(BF16)
    return high, (value - high.astype(F32)).astype(BF16)


def product(left, high, low):
    rows = left.shape[0]
    left_high, left_low = halves(left)
    both = jnp.dot(
        jnp.concatenate([left_high, left_low], axis=0), high, preferred_element_type=F32
    )
    return both[:rows] + both[rows:] + jnp.dot(left_high, low, preferred_element_type=F32)


def kernel(
    src, merge, sweep, out,
    src_stage, merge_stage, sweep_stage, sweep_turned, even_turned,
    state, arrived, from_even, carried, result,
    merge_high, merge_low, sweep_high, sweep_low,
    load_sem, send_sem, recv_sem, even_send, even_recv, op_send, op_recv,
    carry_send, carry_recv, pass_send, pass_recv,
):
    slab = lax.axis_index("slab")
    leaf = lax.axis_index("leaf")
    z, core = lax.div(slab, 2), lax.rem(slab, 2)
    y, x = lax.div(leaf, 4), lax.rem(leaf, 4)
    partner = (
        (slab, y * 4 + x + 1 - 2 * lax.rem(x, 2)),
        (slab, y * 4 + lax.rem(x + 2, 4)),
        (slab, (y + 1 - 2 * lax.rem(y, 2)) * 4 + x),
        (slab, lax.rem(y + 2, 4) * 4 + x),
    )
    sibling = (slab + 1 - 2 * core, leaf)
    late = 1 - core
    blocks = COLS // BLOCK
    per_block = BLOCK // C

    def at_block(block):
        return pl.ds(pl.multiple_of(block * BLOCK, BLOCK), BLOCK)

    def load_source(block):
        return pltpu.make_async_copy(
            src.at[0, 0, :, at_block(block)], src_stage.at[block], load_sem.at[block]
        )

    def load_merge(level):
        return pltpu.make_async_copy(
            merge.at[level, 0, 0], merge_stage.at[level], load_sem.at[blocks + level]
        )

    load_sweep = pltpu.make_async_copy(
        sweep.at[0, 0], sweep_stage, load_sem.at[blocks + LEVELS]
    )

    barrier = pltpu.get_barrier_semaphore()
    for device in (partner[3], partner[1], partner[2], partner[0], sibling):
        pl.semaphore_signal(barrier, inc=1, device_id=device, device_id_type=MESH)

    @pl.when((z > 0) & (core == 1))
    def _():
        pl.semaphore_signal(barrier, inc=1, device_id=(slab - 2, leaf), device_id_type=MESH)

    load_source(0).start()
    load_merge(0).start()
    for block in range(1, blocks):
        load_source(block).start()
    for level in range(1, LEVELS):
        load_merge(level).start()
    load_sweep.start()

    last = lax.div(z + 1, CHIPS)
    pl.semaphore_wait(barrier, 5 + core * (1 - last))

    def rows(chunk):
        return pl.ds(pl.multiple_of(chunk * C, C), C)

    def piece_rows(chunk, piece):
        return pl.ds(pl.multiple_of(chunk * C + piece * PIECE, PIECE), PIECE)

    def exchange(level, chunk):
        return pltpu.make_async_remote_copy(
            src_ref=state.at[level, rows(chunk)],
            dst_ref=arrived.at[level, rows(chunk)],
            send_sem=send_sem.at[level, chunk],
            recv_sem=recv_sem.at[level, chunk],
            device_id=partner[level],
            device_id_type=MESH,
        )

    def to_odd(chunk):
        return pltpu.make_async_remote_copy(
            src_ref=state.at[LEVELS, rows(chunk)],
            dst_ref=from_even.at[rows(chunk)],
            send_sem=even_send.at[chunk],
            recv_sem=even_recv.at[chunk],
            device_id=sibling,
            device_id_type=MESH,
        )

    operator_copy = pltpu.make_async_remote_copy(
        src_ref=sweep_turned,
        dst_ref=even_turned,
        send_sem=op_send,
        recv_sem=op_recv,
        device_id=sibling,
        device_id_type=MESH,
    )

    def carry(chunk, piece):
        return pltpu.make_async_remote_copy(
            src_ref=result.at[piece_rows(chunk, piece)],
            dst_ref=carried.at[piece_rows(chunk, piece)],
            send_sem=carry_send.at[piece, chunk],
            recv_sem=carry_recv.at[piece, chunk],
            device_id=(slab + 2, leaf),
            device_id_type=MESH,
        )

    def pass_on(chunk, piece):
        return pltpu.make_async_remote_copy(
            src_ref=carried.at[piece_rows(chunk, piece)],
            dst_ref=carried.at[piece_rows(chunk, piece)],
            send_sem=pass_send.at[piece, chunk],
            recv_sem=pass_recv.at[piece, chunk],
            device_id=sibling,
            device_id_type=MESH,
        )

    def turn_source(block):
        load_source(block).wait()
        state[0, at_block(block)] = src_stage[block].T

    def prepare_merge(level):
        load_merge(level).wait()

        def turn(step, _):
            at = at_block(step)
            high, low = halves(merge_stage[level, :, at].T)
            merge_high[level, at] = high
            merge_low[level, at] = low
            return 0

        lax.fori_loop(0, 2 * F // BLOCK, turn, 0)

    def prepare_sweep():
        load_sweep.wait()

        def turn(step, _):
            at = at_block(step)
            to = at_block(F // BLOCK + step)
            turned = sweep_stage[:, at].T
            high, low = halves(turned)
            sweep_turned[at] = turned
            sweep_high[at] = high
            sweep_low[at] = low
            sweep_high[to] = high
            sweep_low[to] = low
            return 0

        lax.fori_loop(0, F // BLOCK, turn, 0)

        @pl.when(core == 0)
        def _():
            operator_copy.start()

    def compose_sweep():
        @pl.when(core == 1)
        def _():
            operator_copy.wait_recv()

            def compose(step, _):
                at = at_block(step)
                to = at_block(F // BLOCK + step)
                high, low = halves(product(even_turned[at], sweep_high[:F], sweep_low[:F]))
                sweep_high[to] = high
                sweep_low[to] = low
                return 0

            lax.fori_loop(0, F // BLOCK, compose, 0)

    for block in range(-(-AHEAD * C // BLOCK)):
        turn_source(block)
    for chunk in range(AHEAD):
        exchange(0, chunk).start()
    prepare_merge(0)

    def step(k, _):
        for level in range(1, LEVELS):
            pl.when(k == level - 1)(functools.partial(prepare_merge, level))
        pl.when(k == LEVELS - 2)(prepare_sweep)
        pl.when(k == LEVELS - 1)(compose_sweep)

        ahead = k + AHEAD

        @pl.when((ahead < N) & (lax.rem(ahead, per_block) == 0))
        def _():
            turn_source(lax.div(ahead, per_block))

        for level in range(LEVELS):
            chunk = k - level - late * (level // (LEVELS - 1))

            @pl.when((chunk >= 0) & (chunk < N))
            def _():
                own = product(
                    state[level, rows(chunk)], merge_high[level, :F], merge_low[level, :F]
                )
                exchange(level, chunk).wait_recv()
                state[level + 1, rows(chunk)] = own + product(
                    arrived[level, rows(chunk)], merge_high[level, F:], merge_low[level, F:]
                )
                if level < LEVELS - 1:
                    exchange(level + 1, chunk).start()
                else:
                    @pl.when(core == 0)
                    def _():
                        to_odd(chunk).start()

                if level > 0:
                    exchange(level - 1, chunk).wait_send()

            if level == 0:
                @pl.when(ahead < N)
                def _():
                    exchange(0, ahead).start()

        chunk = k - LEVELS - late

        @pl.when((chunk >= 0) & (chunk < N))
        def _():
            result[rows(chunk)] = product(
                state[LEVELS, rows(chunk)], sweep_high[:F], sweep_low[:F]
            )

            @pl.when(core == 1)
            def _():
                to_odd(chunk).wait_recv()
                result[rows(chunk)] += product(
                    from_even[rows(chunk)], sweep_high[F:], sweep_low[F:]
                )

                @pl.when(z == 0)
                def _():
                    for piece in range(PIECES):
                        carry(chunk, piece).start()

            exchange(LEVELS - 1, chunk).wait_send()

            @pl.when(core == 0)
            def _():
                to_odd(chunk).wait_send()

        chunk = k - LEVELS - late - z
        inside = (chunk >= 0) & (chunk < N)

        @pl.when(inside & (z > 0))
        def _():
            for piece in range(PIECES):
                @pl.when(core == 1)
                def _():
                    carry(chunk, piece).wait_recv()
                    pass_on(chunk, piece).start()

                @pl.when(core == 0)
                def _():
                    pass_on(chunk, piece).wait_recv()

                at = piece_rows(chunk, piece)
                result[at] += product(carried[at], sweep_high[F:], sweep_low[F:])

                @pl.when((core == 1) & (z < CHIPS - 1))
                def _():
                    carry(chunk, piece).start()

        @pl.when(inside & (lax.rem(chunk, per_block) == per_block - 1))
        def _():
            block = lax.div(chunk, per_block)
            out[:, at_block(block)] = result[at_block(block)].T

        def settle(chunk):
            for piece in range(PIECES):
                @pl.when((core == 1) & (z < CHIPS - 1))
                def _():
                    carry(chunk, piece).wait_send()

                @pl.when((core == 1) & (z > 0))
                def _():
                    pass_on(chunk, piece).wait_send()

        @pl.when((chunk >= 1) & (chunk < N))
        def _():
            settle(chunk - 1)

        @pl.when(chunk == N - 1)
        def _():
            settle(chunk)

        return 0

    lax.fori_loop(0, N + LEVELS + late + z, step, 0)

    @pl.when(core == 0)
    def _():
        operator_copy.wait_send()


def per_device(sources, merge_ops, sweep_ops):
    anywhere = pl.BlockSpec(memory_space=pl.ANY)
    dma = pltpu.SemaphoreType.DMA
    whole = pltpu.VMEM((COLS, F), F32)
    square = pltpu.VMEM((F, F), F32)
    blocks = COLS // BLOCK
    interface = pl.pallas_call(
        kernel,
        out_shape=jax.ShapeDtypeStruct((F, COLS), F32),
        in_specs=[pl.BlockSpec(memory_space=pltpu.HBM)] * 3,
        out_specs=pl.BlockSpec(memory_space=pltpu.VMEM),
        scratch_shapes=[
            pltpu.VMEM((blocks, F, BLOCK), F32),
            pltpu.VMEM((LEVELS, F, 2 * F), F32),
            square,
            square,
            square,
            pltpu.VMEM((LEVELS + 1, COLS, F), F32),
            pltpu.VMEM((LEVELS, COLS, F), F32),
            whole,
            whole,
            whole,
            pltpu.VMEM((LEVELS, 2 * F, F), BF16),
            pltpu.VMEM((LEVELS, 2 * F, F), BF16),
            pltpu.VMEM((2 * F, F), BF16),
            pltpu.VMEM((2 * F, F), BF16),
            dma((blocks + LEVELS + 1,)),
            dma((LEVELS, N)),
            dma((LEVELS, N)),
            dma((N,)),
            dma((N,)),
            dma,
            dma,
            dma((PIECES, N)),
            dma((PIECES, N)),
            dma((PIECES, N)),
            dma((PIECES, N)),
        ],
        compiler_params=pltpu.CompilerParams(
            collective_id=0, has_side_effects=True, vmem_limit_bytes=50 << 20
        ),
        cost_estimate=pl.CostEstimate(
            flops=3 * 10 * F * F * COLS, bytes_accessed=15 << 20, transcendentals=0
        ),
        name="solve",
    )(*(pltpu.with_memory_space_constraint(each, pltpu.HBM) for each in (sources, merge_ops, sweep_ops)))
    return interface[None, None]


def solution(mesh):
    in_specs = (
        P("slab", "leaf", None, None),
        P(None, "slab", "leaf", None, None),
        P("slab", "leaf", None, None),
    )
    out_specs = P("slab", "leaf", None, None)
    return jax.shard_map(
        per_device, mesh=mesh, in_specs=in_specs, out_specs=out_specs, check_vma=False
    )
```
